32 devices in a mesh: groups: 2 (over y), seq: 4 (over z), head: 2 (over x), rep: 2 (over core).
Axes of the slice: x: 2, y: 2, z: 4, core: 2. Of those that a mesh axis runs over, the one named last changes fastest.
Arguments:
- queries: bfloat16 [32768, 16, 128], P(('groups', 'seq'), ('head', 'rep')), parts along dimension 0, may hold values from -8 to 8
- keys: bfloat16 [32768, 128], P(('groups', 'seq')), parts along dimension 0, may hold values from -6 to 6
- values: bfloat16 [32768, 128], P(('groups', 'seq')), parts along dimension 0, may hold values from -6 to 6
- query_maps: bfloat16 [32, 128, 128], P(('groups', 'head', 'rep')), parts along dimension 0, may hold values from -0.5 to 0.5
- key_map: bfloat16 [256, 128], P('groups'), parts along dimension 0, may hold values from -0.046875 to 0.046875
- linear_cotangent: bfloat16 [32768, 16, 128], P(('groups', 'seq'), ('head', 'rep')), parts along dimension 0, may hold values from -0.046875 to 0.046875
Outputs:
- softmax_out: bfloat16 [32768, 16, 128], P(('groups', 'seq'), ('head', 'rep')), parts along dimension 0
- linear_out: bfloat16 [32768, 16, 128], P(('groups', 'seq'), ('head', 'rep')), parts along dimension 0
- map_gradient: float32 [256, 16, 128], P(('groups', 'seq'), ('head', 'rep')), parts along dimension 0
The draws below stay inside these ranges and needn't reach their ends.
There are 2 independent parts, one for each index of `groups`. The reference program is written for one: setup_inputs(seed, part) draws one part's arguments, and reference() takes and returns one part's arrays. A program takes and returns all parts, laid end to end along the dimension named above; each array names one. Nothing has to cross between parts.
All inputs are finite; a program needn't handle non-finite values.
Results may differ from the reference program's by a relative error of at most 0.0058.
Values may be sent and summed in bfloat16 or wider, within the bound.
A program may use at most 128 MiB of HBM per device.

```python
import jax
import jax.numpy as jnp
from jax import lax

H = 16
HD = 128
W = 512
TOKENS = 16384


def draw_keys(key, part):
    drawn = jnp.clip(jax.random.normal(jax.random.fold_in(key, 11), (TOKENS, HD), jnp.float32), -6.0, 6.0)
    return drawn.astype(jnp.bfloat16)


def draw_queries(key, part):
    drawn = jnp.clip(jax.random.normal(jax.random.fold_in(key, 21), (TOKENS, H, HD), jnp.float32), -6.0, 6.0)
    return drawn.astype(jnp.bfloat16)


def block_scale(own_key, extent, cuts, least, largest):
    gain, own = 1.0, jax.random.fold_in(own_key, 6)
    for position, blocks in cuts:
        draws = jnp.exp(jax.random.uniform(jax.random.fold_in(own, position), (blocks,), jnp.float32, least / len(cuts), largest / len(cuts)))
        gain = gain * jnp.repeat(draws, extent[position] // blocks).reshape([-1 if axis == position else 1 for axis in range(len(extent))])
    return gain


def normal_values(own_key, shape, scale, most, cuts=(), kind=jnp.bfloat16):
    values = scale * jax.random.normal(own_key, shape, jnp.float32)
    if cuts:
        values = values * block_scale(own_key, shape, cuts, -0.22, 0.18)
    return jnp.clip(values, -most, most).astype(kind)


def setup_inputs(seed: int = 0, part: int = 0) -> dict:
    arg_keys = jax.random.split(jax.random.key(seed), 7)
    part_splits = jax.random.split(jax.random.fold_in(arg_keys[6], part), 7)
    queries = draw_queries(jax.random.fold_in(jax.random.fold_in(arg_keys[6], part), 71), part)
    keys = draw_keys(jax.random.fold_in(jax.random.fold_in(arg_keys[6], part), 71), part)
    values = normal_values(part_splits[2], (TOKENS, HD), 1.0, 6.0, ((0, 4),))
    query_maps = normal_values(part_splits[3], (H, HD, HD), HD ** -0.5, 0.5, ((0, 4),))
    key_map = normal_values(part_splits[4], (HD, HD), (HD * HD) ** -0.5, 0.046875)
    linear_cotangent = normal_values(part_splits[5], (TOKENS, H, HD), (1.0 / TOKENS ** 0.5), 0.046875, ((0, 4), (1, 4)))
    return {"queries": queries, "keys": keys, "values": values, "query_maps": query_maps, "key_map": key_map, "linear_cotangent": linear_cotangent}


def window_block(block_index, start_state, tensors):
    queries, keys_ext, values_ext, query_features, key_features, values, cotangent = tensors
    highest_precision = lax.Precision.HIGHEST
    first_row = block_index * W
    head_dim = keys_ext.shape[1]
    query_block = lax.dynamic_slice_in_dim(queries, first_row, W, 0).astype(jnp.float32)
    key_window = lax.dynamic_slice_in_dim(keys_ext, first_row, 2 * W, 0).astype(jnp.float32)
    value_window = lax.dynamic_slice_in_dim(values_ext, first_row, 2 * W, 0).astype(jnp.float32)
    query_pos = first_row + jnp.arange(W, dtype=jnp.int32)
    key_pos = first_row - W + jnp.arange(2 * W, dtype=jnp.int32)
    spacing = query_pos[:, None] - key_pos[None, :]
    allowed = (spacing >= 0) & (spacing < W) & (key_pos[None, :] >= 0)
    scores = jnp.einsum('whd,kd->hwk', query_block, key_window, precision=highest_precision) * head_dim ** (-0.5)
    scores = jnp.where(allowed[None], scores, -1e+30)
    highest = lax.optimization_barrier(jnp.max(scores, axis=2, keepdims=True))
    shifted_exp = jnp.exp(scores - highest)
    weights = (shifted_exp / lax.optimization_barrier(jnp.sum(shifted_exp, axis=2, keepdims=True))).astype(jnp.bfloat16)
    soft_block = jnp.einsum('hwk,kd->whd', weights.astype(jnp.float32), value_window, precision=highest_precision).astype(jnp.bfloat16)
    feature_block = lax.dynamic_slice_in_dim(query_features, first_row, W, 0).astype(jnp.float32)
    key_block = lax.dynamic_slice_in_dim(key_features, first_row, W, 0).astype(jnp.float32)
    value_block = lax.dynamic_slice_in_dim(values, first_row, W, 0).astype(jnp.float32)
    cotangent_block = lax.dynamic_slice_in_dim(cotangent, first_row, W, 0).astype(jnp.float32)
    causal = jnp.arange(W)[:, None] >= jnp.arange(W)[None, :]
    factor = lax.rsqrt((query_pos + 1).astype(jnp.float32))[:, None, None]
    linear_scores = jnp.where(causal[None], jnp.einsum('whf,sf->hws', feature_block, key_block, precision=highest_precision), 0.0).astype(jnp.bfloat16)
    inside = jnp.einsum('hws,sd->whd', linear_scores.astype(jnp.float32), value_block, precision=highest_precision)
    carried = jnp.einsum('whf,fd->whd', feature_block, start_state, precision=highest_precision)
    linear_block = (factor * (inside + carried)).astype(jnp.bfloat16)
    back_scores = jnp.where(causal[None], jnp.einsum('whd,sd->hws', cotangent_block, value_block, precision=highest_precision), 0.0).astype(jnp.bfloat16)
    back_inside = jnp.einsum('hws,sf->whf', back_scores.astype(jnp.float32), key_block, precision=highest_precision)
    back_carried = jnp.einsum('whd,fd->whf', cotangent_block, start_state, precision=highest_precision)
    feature_gradient = (factor * (back_inside + back_carried)).astype(jnp.bfloat16)
    return (soft_block, linear_block, feature_gradient)

def reference(queries, keys, values, query_maps, key_map, linear_cotangent):
    token_count = keys.shape[0]
    head_dim = keys.shape[1]
    head_count = queries.shape[1]
    block_count = token_count // W
    key_features = jnp.dot(keys, key_map, preferred_element_type=jnp.float32).astype(jnp.bfloat16)
    query_features = jnp.einsum('thd,hdf->thf', queries.astype(jnp.float32), query_maps.astype(jnp.float32), precision=lax.Precision.HIGHEST).astype(jnp.bfloat16)
    block_states = jnp.einsum('bwf,bwd->bfd', key_features.reshape(block_count, W, head_dim).astype(jnp.float32), values.reshape(block_count, W, head_dim).astype(jnp.float32), precision=lax.Precision.HIGHEST)
    running = jnp.cumsum(block_states, axis=0)
    starts = jnp.concatenate([jnp.zeros_like(block_states[:1]), running[:-1]], axis=0)
    padding = jnp.zeros((W, head_dim), keys.dtype)
    keys_ext = jnp.concatenate([padding, keys], axis=0)
    values_ext = jnp.concatenate([padding, values], axis=0)
    tensors = (queries, keys_ext, values_ext, query_features, key_features, values, linear_cotangent)

    def one_block(block_item):
        return window_block(block_item[0], block_item[1], tensors)
    soft_parts, linear_parts, gradient_parts = lax.map(one_block, (jnp.arange(block_count, dtype=jnp.int32), starts))
    softmax_out = soft_parts.reshape(token_count, head_count, head_dim)
    linear_out = linear_parts.reshape(token_count, head_count, head_dim)
    feature_gradient = gradient_parts.reshape(token_count, head_count, head_dim)
    map_gradient = jnp.einsum('the,thf->ehf', queries.astype(jnp.float32), feature_gradient.astype(jnp.float32), precision=lax.Precision.HIGHEST)
    return (softmax_out, linear_out, map_gradient)
```

```python
import functools

import jax
import jax.numpy as jnp
from jax import lax
from jax.experimental import pallas as pl
from jax.experimental.pallas import tpu as pltpu
from jax.sharding import PartitionSpec as P

W = 512
TILE = 128


def from_behind(value, axis, steps):
    count = lax.axis_size(axis)
    return lax.ppermute(value, axis, [(s, s + steps) for s in range(count - steps)])


def nt(a, b):
    return lax.dot_general(a, b, (((1,), (1,)), ((), ())), preferred_element_type=jnp.float32)


def tn(a, b):
    return lax.dot_general(a, b, (((0,), (0,)), ((), ())), preferred_element_type=jnp.float32)


def nn(a, b):
    return jnp.dot(a, b, preferred_element_type=jnp.float32)


def split_two(x):
    high = x.astype(jnp.bfloat16)
    return high, (x - high.astype(jnp.float32)).astype(jnp.bfloat16)


def main_kernel(
    tokens_here, heads, tiles, rows_sub,
    q_ref, c_ref, k_ref, v_ref, rim_k_ref, rim_v_ref, key_map_ref, maps_ref, prefix_ref,
    soft_ref, linear_ref, grad_ref,
    k_ext, v_ext, kf_all, head_mask, state,
):
    step = pl.program_id(0)
    rank = lax.axis_index("seq")
    hd = q_ref.shape[1]
    rows = TILE * heads

    @pl.when(step == 0)
    def _():
        k_ext[:W] = rim_k_ref[...]
        k_ext[W:] = k_ref[...]
        v_ext[:W, :hd] = rim_v_ref[...]
        v_ext[W:, :hd] = v_ref[...]
        v_ext[:, hd:] = jnp.ones((v_ext.shape[0], hd), jnp.bfloat16)
        kf_all[...] = nn(k_ref[...], key_map_ref[...]).astype(jnp.bfloat16)
        row = lax.broadcasted_iota(jnp.int32, head_mask.shape, 0) % heads
        column = lax.broadcasted_iota(jnp.int32, head_mask.shape, 1) // hd
        head_mask[...] = jnp.where(row == column, 1.0, 0.0).astype(jnp.bfloat16)
        state[...] = prefix_ref[...]
        grad_ref[...] = jnp.zeros_like(grad_ref)

    scale = hd ** (-0.5) * 1.4426950408889634
    zero = jnp.zeros((TILE, hd), jnp.bfloat16)
    mids = W // TILE
    for tile in range(tiles):
        index = step * tiles + tile
        first = pl.multiple_of(index * TILE, TILE)
        k_win = k_ext[pl.ds(first, W + TILE), :]
        v_win = v_ext[pl.ds(first, W + TILE), :]
        kf = kf_all[pl.ds(first, TILE), :]
        v = v_ref[pl.ds(first, TILE), :]
        s_now = state[...]
        s_hi, s_lo = split_two(s_now)
        t_hi, t_lo = split_two(s_now.T)

        def diagonal(a, b):
            return jnp.concatenate(
                [jnp.concatenate([a, zero], 1), jnp.concatenate([zero, b], 1)], 0
            )

        into_scores = diagonal(kf, v)
        from_scores = jnp.concatenate([diagonal(v, kf), diagonal(s_hi, t_hi), diagonal(s_lo, t_lo)], 0)
        invalid = [
            jnp.where((rank == 0) & (index + j < mids), -1e30, 0.0).astype(jnp.float32)
            for j in range(mids)
        ]
        gradients = []
        for sub in range(rows // rows_sub):
            start = tile * rows + sub * rows_sub
            q = q_ref[start : start + rows_sub, :]
            c = c_ref[start : start + rows_sub, :]
            shape = (rows_sub, TILE)
            local = (lax.broadcasted_iota(jnp.int32, shape, 0) + sub * rows_sub) // heads
            ahead = lax.broadcasted_iota(jnp.int32, shape, 1) > local
            scores = nt(q, k_win)
            parts = [scores[:, j * TILE : (j + 1) * TILE] for j in range(mids + 1)]
            parts = [p + invalid[j] if j < mids else p for j, p in enumerate(parts)]
            both = jnp.where(ahead, parts[0], parts[mids])
            kept = [both] + parts[1:mids]
            highest = jnp.max(functools.reduce(jnp.maximum, kept), axis=1, keepdims=True)
            kept = [jnp.exp2((p - highest) * scale) for p in kept]
            weights = jnp.concatenate(
                [jnp.where(ahead, kept[0], 0.0).astype(jnp.bfloat16)]
                + [p.astype(jnp.bfloat16) for p in kept[1:]]
                + [jnp.where(ahead, 0.0, kept[0]).astype(jnp.bfloat16)], 1
            )
            soft = nn(weights, v_win)
            soft_ref[start : start + rows_sub, :] = (soft[:, :hd] / soft[:, hd:]).astype(jnp.bfloat16)
            mask = head_mask[...]
            q_heads = jnp.concatenate([q] * heads, 1) * mask
            qf = nn(q_heads, maps_ref[...]).astype(jnp.bfloat16)
            pair = jnp.concatenate([qf, c], 1)
            pair_scores = nt(pair, into_scores)
            ahead_two = jnp.concatenate([ahead, ahead], 1)
            pair_scores = jnp.where(ahead_two, 0.0, pair_scores).astype(jnp.bfloat16)
            pair_out = nn(jnp.concatenate([pair_scores, pair, pair], 1), from_scores)
            position = rank * tokens_here + index * TILE + local + 1
            factor = lax.rsqrt(position.astype(jnp.float32))
            linear_ref[start : start + rows_sub, :] = (factor * pair_out[:, :hd]).astype(jnp.bfloat16)
            fg = (factor * pair_out[:, hd:]).astype(jnp.bfloat16)
            gradients.append(jnp.concatenate([fg] * heads, 1) * mask)
        grad_ref[...] += tn(
            q_ref[tile * rows : (tile + 1) * rows, :], jnp.concatenate(gradients, 0)
        )
        state[...] = s_now + tn(kf, v)


def per_device(queries, keys, values, query_maps, key_map, linear_cotangent):
    tokens_here, head_dim = keys.shape
    heads = queries.shape[1]
    count = lax.axis_size("seq")
    rank = lax.axis_index("seq")
    rim_keys, rim_values = from_behind(
        (keys[tokens_here - W :], values[tokens_here - W :]), "seq", 1
    )
    key_features = jnp.dot(keys, key_map, preferred_element_type=jnp.float32).astype(jnp.bfloat16)
    local_sum = lax.dot_general(
        key_features, values, (((0,), (0,)), ((), ())), preferred_element_type=jnp.float32
    )
    prefix = jnp.zeros_like(local_sum)
    for k in range(1, count):
        prefix = prefix + from_behind(local_sum, "seq", k)

    tiles = 4
    rows_sub = min(256, TILE * heads)
    step_rows = TILE * tiles * heads
    total = tokens_here * heads
    whole = lambda a: pl.BlockSpec(a.shape, lambda i: (0,) * a.ndim)
    rows_spec = pl.BlockSpec((step_rows, head_dim), lambda i: (i, 0))
    maps = query_maps.reshape(heads * head_dim, head_dim)
    soft, linear, grad = pl.pallas_call(
        functools.partial(main_kernel, tokens_here, heads, tiles, rows_sub),
        grid=(total // step_rows,),
        in_specs=[rows_spec, rows_spec]
        + [whole(a) for a in (keys, values, rim_keys, rim_values, key_map, maps, prefix)],
        out_specs=[rows_spec, rows_spec, pl.BlockSpec((head_dim, heads * head_dim), lambda i: (0, 0))],
        out_shape=[
            jax.ShapeDtypeStruct((total, head_dim), jnp.bfloat16),
            jax.ShapeDtypeStruct((total, head_dim), jnp.bfloat16),
            jax.ShapeDtypeStruct((head_dim, heads * head_dim), jnp.float32),
        ],
        scratch_shapes=[
            pltpu.VMEM((tokens_here + W, head_dim), jnp.bfloat16),
            pltpu.VMEM((tokens_here + W, 2 * head_dim), jnp.bfloat16),
            pltpu.VMEM((tokens_here, head_dim), jnp.bfloat16),
            pltpu.VMEM((rows_sub, heads * head_dim), jnp.bfloat16),
            pltpu.VMEM((head_dim, head_dim), jnp.float32),
        ],
        compiler_params=pltpu.CompilerParams(dimension_semantics=("arbitrary",)),
        name="attention",
    )(
        queries.reshape(total, head_dim), linear_cotangent.reshape(total, head_dim),
        keys, values, rim_keys, rim_values, key_map, maps, prefix,
    )
    share = head_dim // count
    piece = lambda k: lax.dynamic_slice_in_dim(grad, ((rank + k) % count) * share, share, 0)
    mine = piece(0)
    for k in range(1, count):
        mine = mine + lax.ppermute(piece(k), "seq", [(s, (s + k) % count) for s in range(count)])
    shape = (tokens_here, heads, head_dim)
    return soft.reshape(shape), linear.reshape(shape), mine.reshape(share, heads, head_dim)


def solution(mesh):
    rows = P(("groups", "seq"), ("head", "rep"), None)
    return jax.shard_map(
        per_device,
        mesh=mesh,
        in_specs=(
            rows,
            P(("groups", "seq"), None),
            P(("groups", "seq"), None),
            P(("groups", "head", "rep"), None, None),
            P("groups", None),
            rows,
        ),
        out_specs=(rows, rows, rows),
        check_vma=False,
    )
```

```python
import functools

import jax
import jax.numpy as jnp
from jax import lax
from jax.experimental import pallas as pl
from jax.experimental.pallas import tpu as pltpu
from jax.sharding import PartitionSpec as P

W = 512
TILE = 128
MESH = pl.DeviceIdType.MESH


def nt(a, b):
    return lax.dot_general(a, b, (((1,), (1,)), ((), ())), preferred_element_type=jnp.float32)


def tn(a, b):
    return lax.dot_general(a, b, (((0,), (0,)), ((), ())), preferred_element_type=jnp.float32)


def nn(a, b):
    return jnp.dot(a, b, preferred_element_type=jnp.float32)


def split_two(x):
    high = x.astype(jnp.bfloat16)
    return high, (x - high.astype(jnp.float32)).astype(jnp.bfloat16)


def head_masks(rows, heads, inner, hd):
    def mask(parts, of_head):
        shape = (rows, parts * hd)
        head = lax.broadcasted_iota(jnp.int32, shape, 0) % heads
        part = lax.broadcasted_iota(jnp.int32, shape, 1) // hd
        return jnp.where(of_head(head) == part, 1.0, 0.0).astype(jnp.bfloat16)

    return mask(heads // inner, lambda h: h // inner), mask(inner, lambda h: h % inner)


def seq_barrier(rank, count):
    barrier = pltpu.get_barrier_semaphore()
    for k in range(1, count):
        pl.semaphore_signal(
            barrier, inc=1, device_id={"seq": lax.rem(rank + k, count)}, device_id_type=MESH
        )
    return barrier


def first_kernel(
    count, heads, inner, steps,
    q_ref, maps_ref, k_ref, v_ref, key_map_ref,
    qf_ref, kf_ref, rim_k_ref, rim_v_ref, prefix_ref,
    outer_mask, local_sum, sums, halo, sum_send, sum_recv, halo_send, halo_recv,
):
    step = pl.program_id(0)
    rank = lax.axis_index("seq")
    tokens, hd = k_ref.shape
    rows = outer_mask.shape[0]

    def halo_copy(i):
        return pltpu.make_async_remote_copy(
            src_ref=(k_ref, v_ref)[i].at[pl.ds(tokens - W, W)],
            dst_ref=halo.at[i],
            send_sem=halo_send.at[i],
            recv_sem=halo_recv.at[i],
            device_id={"seq": rank + 1},
            device_id_type=MESH,
        )

    def sum_copy(k):
        return pltpu.make_async_remote_copy(
            src_ref=local_sum,
            dst_ref=sums.at[k - 1],
            send_sem=sum_send.at[k - 1],
            recv_sem=sum_recv.at[k - 1],
            device_id={"seq": rank + k},
            device_id_type=MESH,
        )

    @pl.when(step == 0)
    def _():
        barrier = seq_barrier(rank, count)
        kf_ref[...] = nn(k_ref[...], key_map_ref[...]).astype(jnp.bfloat16)
        local_sum[...] = tn(kf_ref[...], v_ref[...])
        outer_mask[...] = head_masks(rows, heads, inner, hd)[0]
        pl.semaphore_wait(barrier, count - 1)
        for k in range(1, count):
            @pl.when(rank + k < count)
            def _():
                sum_copy(k).start()
        @pl.when(rank + 1 < count)
        def _():
            halo_copy(0).start()
            halo_copy(1).start()

    outer = heads // inner
    maps = jnp.concatenate(
        [
            jnp.concatenate([maps_ref[(a * inner + b) * hd : (a * inner + b + 1) * hd] for b in range(inner)], 1)
            for a in range(outer)
        ], 0
    )
    inner_head = lax.broadcasted_iota(jnp.int32, (rows, hd), 0) % inner
    for start in range(0, q_ref.shape[0], rows):
        q = q_ref[start : start + rows, :]
        spread = nn(jnp.concatenate([q] * outer, 1) * outer_mask[...], maps)
        qf = spread[:, :hd]
        for b in range(1, inner):
            qf = jnp.where(inner_head == b, spread[:, b * hd : (b + 1) * hd], qf)
        qf_ref[start : start + rows, :] = qf.astype(jnp.bfloat16)

    @pl.when(step == steps - 1)
    def _():
        prefix_ref[...] = jnp.zeros_like(prefix_ref)
        for k in range(1, count):
            @pl.when(rank + k < count)
            def _():
                sum_copy(k).wait_send()
            @pl.when(rank >= k)
            def _():
                sum_copy(k).wait_recv()
                prefix_ref[...] += sums[k - 1]
        @pl.when(rank + 1 < count)
        def _():
            halo_copy(0).wait_send()
            halo_copy(1).wait_send()
        @pl.when(rank >= 1)
        def _():
            halo_copy(0).wait_recv()
            halo_copy(1).wait_recv()
            rim_k_ref[...] = halo[0]
            rim_v_ref[...] = halo[1]
        @pl.when(rank == 0)
        def _():
            rim_k_ref[...] = jnp.zeros_like(rim_k_ref)
            rim_v_ref[...] = jnp.zeros_like(rim_v_ref)


def last_kernel(count, g_ref, g16_ref, out_ref, slots, send_sem, recv_sem):
    rank = lax.axis_index("seq")
    barrier = seq_barrier(rank, count)
    pl.semaphore_wait(barrier, count - 1)
    copies = []
    for k in range(1, count):
        target = lax.rem(rank + k, count)
        copies.append(pltpu.make_async_remote_copy(
            src_ref=g16_ref.at[target],
            dst_ref=slots.at[k - 1],
            send_sem=send_sem.at[k - 1],
            recv_sem=recv_sem.at[k - 1],
            device_id={"seq": target},
            device_id_type=MESH,
        ))
    for copy in copies:
        copy.start()
    total = g_ref[rank]
    for k, copy in enumerate(copies):
        copy.wait()
        total = total + slots[k].astype(jnp.float32)
    out_ref[...] = total


def main_kernel(
    tokens_here, heads, inner, tiles, rows_sub, steps,
    q_ref, qf_ref, c_ref, k_ref, v_ref, kf_ref, rim_k_ref, rim_v_ref, prefix_ref,
    soft_ref, linear_ref, grad_ref, grad16_ref,
    k_ext, v_ext, outer_mask, inner_mask, state, grad,
):
    step = pl.program_id(0)
    rank = lax.axis_index("seq")
    hd = q_ref.shape[1]
    rows = TILE * heads
    outer = heads // inner

    @pl.when(step == 0)
    def _():
        k_ext[:W] = rim_k_ref[...]
        k_ext[W:] = k_ref[...]
        v_ext[:W, :hd] = rim_v_ref[...]
        v_ext[W:, :hd] = v_ref[...]
        v_ext[:, hd:] = jnp.ones((v_ext.shape[0], hd), jnp.bfloat16)
        outer_mask[...], inner_mask[...] = head_masks(rows_sub, heads, inner, hd)
        state[...] = prefix_ref[...]
        grad[...] = jnp.zeros_like(grad)

    scale = hd ** (-0.5) * 1.4426950408889634
    zero = jnp.zeros((TILE, hd), jnp.bfloat16)
    mids = W // TILE
    for tile in range(tiles):
        index = step * tiles + tile
        first = pl.multiple_of(index * TILE, TILE)
        k_win = k_ext[pl.ds(first, W + TILE), :]
        v_win = v_ext[pl.ds(first, W + TILE), :]
        kf = kf_ref[pl.ds(first, TILE), :]
        v = v_ref[pl.ds(first, TILE), :]
        s_now = state[...]
        s_hi, s_lo = split_two(s_now)
        t_hi, t_lo = split_two(s_now.T)

        def diagonal(a, b):
            return jnp.concatenate(
                [jnp.concatenate([a, zero], 1), jnp.concatenate([zero, b], 1)], 0
            )

        into_scores = diagonal(kf, v)
        from_scores = jnp.concatenate([diagonal(v, kf), diagonal(s_hi, t_hi), diagonal(s_lo, t_lo)], 0)
        invalid = [
            jnp.where((rank == 0) & (index + j < mids), -1e30, 0.0).astype(jnp.float32)
            for j in range(mids)
        ]
        queries, gradients = [], []
        for sub in range(rows // rows_sub):
            start = tile * rows + sub * rows_sub
            q = q_ref[start : start + rows_sub, :]
            c = c_ref[start : start + rows_sub, :]
            shape = (rows_sub, TILE)
            local = (lax.broadcasted_iota(jnp.int32, shape, 0) + sub * rows_sub) // heads
            ahead = lax.broadcasted_iota(jnp.int32, shape, 1) > local
            scores = nt(q, k_win)
            parts = [scores[:, j * TILE : (j + 1) * TILE] for j in range(mids + 1)]
            parts = [p + invalid[j] if j < mids else p for j, p in enumerate(parts)]
            both = jnp.where(ahead, parts[0], parts[mids])
            kept = [both] + parts[1:mids]
            highest = jnp.max(functools.reduce(jnp.maximum, kept), axis=1, keepdims=True)
            kept = [jnp.exp2((p - highest) * scale) for p in kept]
            weights = jnp.concatenate(
                [jnp.where(ahead, kept[0], 0.0).astype(jnp.bfloat16)]
                + [p.astype(jnp.bfloat16) for p in kept[1:]]
                + [jnp.where(ahead, 0.0, kept[0]).astype(jnp.bfloat16)], 1
            )
            soft = nn(weights, v_win)
            soft_ref[start : start + rows_sub, :] = (soft[:, :hd] / soft[:, hd:]).astype(jnp.bfloat16)
            pair = jnp.concatenate([qf_ref[start : start + rows_sub, :], c], 1)
            pair_scores = nt(pair, into_scores)
            ahead_two = jnp.concatenate([ahead, ahead], 1)
            pair_scores = jnp.where(ahead_two, 0.0, pair_scores).astype(jnp.bfloat16)
            pair_out = nn(jnp.concatenate([pair_scores, pair, pair], 1), from_scores)
            position = rank * tokens_here + index * TILE + local + 1
            factor = lax.rsqrt(position.astype(jnp.float32))
            linear_ref[start : start + rows_sub, :] = (factor * pair_out[:, :hd]).astype(jnp.bfloat16)
            fg = (factor * pair_out[:, hd:]).astype(jnp.bfloat16)
            queries.append(jnp.concatenate([q] * outer, 1) * outer_mask[...])
            gradients.append(jnp.concatenate([fg] * inner, 1) * inner_mask[...])
        grad[...] += tn(jnp.concatenate(queries, 0), jnp.concatenate(gradients, 0))
        state[...] = s_now + tn(kf, v)

    @pl.when(step == steps - 1)
    def _():
        for a in range(outer):
            block = grad[a * hd : (a + 1) * hd, :]
            block = block.reshape(grad_ref.shape[:2] + (inner * hd,))
            grad_ref[:, :, a * inner * hd : (a + 1) * inner * hd] = block
            grad16_ref[:, :, a * inner * hd : (a + 1) * inner * hd] = block.astype(jnp.bfloat16)


def per_device(queries, keys, values, query_maps, key_map, linear_cotangent):
    tokens_here, hd = keys.shape
    heads = queries.shape[1]
    count = lax.axis_size("seq")
    inner = 2 if heads % 2 == 0 else 1
    outer = heads // inner
    share = hd // count
    tiles = 4
    rows_sub = min(256, TILE * heads)
    step_rows = TILE * tiles * heads
    total = tokens_here * heads
    steps = total // step_rows
    whole = lambda a: pl.BlockSpec(a.shape, lambda i: (0,) * len(a.shape))
    rows_spec = pl.BlockSpec((step_rows, hd), lambda i: (i, 0))
    maps = query_maps.reshape(heads * hd, hd)
    queries = queries.reshape(total, hd)
    cotangent = linear_cotangent.reshape(total, hd)

    rows16 = jax.ShapeDtypeStruct((total, hd), jnp.bfloat16)
    kf16 = jax.ShapeDtypeStruct((tokens_here, hd), jnp.bfloat16)
    rim = jax.ShapeDtypeStruct((W, hd), jnp.bfloat16)
    square = jax.ShapeDtypeStruct((hd, hd), jnp.float32)
    dma = pltpu.SemaphoreType.DMA
    query_features, key_features, rim_keys, rim_values, prefix = pl.pallas_call(
        functools.partial(first_kernel, count, heads, inner, steps),
        grid=(steps,),
        in_specs=[rows_spec] + [whole(a) for a in (maps, keys, values, key_map)],
        out_specs=[rows_spec] + [whole(a) for a in (kf16, rim, rim, square)],
        out_shape=[rows16, kf16, rim, rim, square],
        scratch_shapes=[
            pltpu.VMEM((rows_sub, outer * hd), jnp.bfloat16),
            pltpu.VMEM((hd, hd), jnp.float32),
            pltpu.VMEM((count - 1, hd, hd), jnp.float32),
            pltpu.VMEM((2, W, hd), jnp.bfloat16),
            dma((count - 1,)), dma((count - 1,)), dma((2,)), dma((2,)),
        ],
        compiler_params=pltpu.CompilerParams(
            dimension_semantics=("arbitrary",), collective_id=0, has_side_effects=True
        ),
        name="features",
    )(queries, maps, keys, values, key_map)

    pieces = (count, share, heads * hd)
    small = (keys, values, key_features, rim_keys, rim_values, prefix)
    soft, linear, grad, grad16 = pl.pallas_call(
        functools.partial(main_kernel, tokens_here, heads, inner, tiles, rows_sub, steps),
        grid=(steps,),
        in_specs=[rows_spec] * 3 + [whole(a) for a in small],
        out_specs=[rows_spec] * 2 + [pl.BlockSpec(pieces, lambda i: (0, 0, 0))] * 2,
        out_shape=[
            rows16, rows16,
            jax.ShapeDtypeStruct(pieces, jnp.float32),
            jax.ShapeDtypeStruct(pieces, jnp.bfloat16),
        ],
        scratch_shapes=[
            pltpu.VMEM((tokens_here + W, hd), jnp.bfloat16),
            pltpu.VMEM((tokens_here + W, 2 * hd), jnp.bfloat16),
            pltpu.VMEM((rows_sub, outer * hd), jnp.bfloat16),
            pltpu.VMEM((rows_sub, inner * hd), jnp.bfloat16),
            pltpu.VMEM((hd, hd), jnp.float32),
            pltpu.VMEM((outer * hd, inner * hd), jnp.float32),
        ],
        compiler_params=pltpu.CompilerParams(dimension_semantics=("arbitrary",)),
        name="attention",
    )(queries, query_features, cotangent, *small)

    vmem = pl.BlockSpec(memory_space=pltpu.VMEM)
    mine = pl.pallas_call(
        functools.partial(last_kernel, count),
        in_specs=[vmem, vmem],
        out_specs=vmem,
        out_shape=jax.ShapeDtypeStruct(pieces[1:], jnp.float32),
        scratch_shapes=[
            pltpu.VMEM((count - 1,) + pieces[1:], jnp.bfloat16), dma((count - 1,)), dma((count - 1,)),
        ],
        compiler_params=pltpu.CompilerParams(collective_id=1, has_side_effects=True),
        name="map_gradient",
    )(grad, grad16)
    shape = (tokens_here, heads, hd)
    return soft.reshape(shape), linear.reshape(shape), mine.reshape(share, heads, hd)


def solution(mesh):
    rows = P(("groups", "seq"), ("head", "rep"), None)
    return jax.shard_map(
        per_device,
        mesh=mesh,
        in_specs=(
            rows,
            P(("groups", "seq"), None),
            P(("groups", "seq"), None),
            P(("groups", "head", "rep"), None, None),
            P("groups", None),
            rows,
        ),
        out_specs=(rows, rows, rows),
        check_vma=False,
    )
```

```python
import functools

import jax
import jax.numpy as jnp
from jax import lax
from jax.experimental import pallas as pl
from jax.experimental.pallas import tpu as pltpu
from jax.sharding import PartitionSpec as P

W = 512
TILE = 128
MESH = pl.DeviceIdType.MESH


def nt(a, b):
    return lax.dot_general(a, b, (((1,), (1,)), ((), ())), preferred_element_type=jnp.float32)


def tn(a, b):
    return lax.dot_general(a, b, (((0,), (0,)), ((), ())), preferred_element_type=jnp.float32)


def nn(a, b):
    return jnp.dot(a, b, preferred_element_type=jnp.float32)


def head_masks(rows, heads, inner, hd):
    def mask(parts, of_head):
        shape = (rows, parts * hd)
        head = lax.broadcasted_iota(jnp.int32, shape, 0) % heads
        part = lax.broadcasted_iota(jnp.int32, shape, 1) // hd
        return jnp.where(of_head(head) == part, 1.0, 0.0).astype(jnp.bfloat16)

    return mask(heads // inner, lambda h: h // inner), mask(inner, lambda h: h % inner)


def ahead_of(rows, start, heads):
    shape = (rows, TILE)
    local = (lax.broadcasted_iota(jnp.int32, shape, 0) + start) // heads
    return local, lax.broadcasted_iota(jnp.int32, shape, 1) > local


def window_softmax(q, k_win, v_win, ahead, invalid=None):
    hd = q.shape[1]
    mids = W // TILE
    scale = hd ** (-0.5) * 1.4426950408889634
    scores = nt(q, k_win)
    parts = [scores[:, j * TILE : (j + 1) * TILE] for j in range(mids + 1)]
    if invalid is not None:
        parts = [p + invalid[j] if j < mids else p for j, p in enumerate(parts)]
    kept = [jnp.where(ahead, parts[0], parts[mids])] + parts[1:mids]
    highest = jnp.max(functools.reduce(jnp.maximum, kept), axis=1, keepdims=True)
    kept = [jnp.exp2((p - highest) * scale) for p in kept]
    weights = jnp.concatenate(
        [jnp.where(ahead, kept[0], 0.0).astype(jnp.bfloat16)]
        + [p.astype(jnp.bfloat16) for p in kept[1:]]
        + [jnp.where(ahead, 0.0, kept[0]).astype(jnp.bfloat16)], 1
    )
    soft = nn(weights, v_win)
    return (soft[:, :hd] / soft[:, hd:]).astype(jnp.bfloat16)


def seq_barrier(rank, count):
    barrier = pltpu.get_barrier_semaphore()
    for k in range(1, count):
        pl.semaphore_signal(
            barrier, inc=1, device_id={"seq": lax.rem(rank + k, count)}, device_id_type=MESH
        )
    return barrier


def first_kernel(
    count, heads, inner, steps, late_tile,
    q_ref, late_q_ref, maps_ref, k_ref, v_ref, key_map_ref,
    qf_ref, late_soft_ref, kf_ref, rim_k_ref, rim_v_ref, prefix_ref,
    v_ones, outer_mask, local_sum, sums, halo, sum_send, sum_recv, halo_send, halo_recv,
):
    step = pl.program_id(0)
    rank = lax.axis_index("seq")
    tokens, hd = k_ref.shape
    rows = outer_mask.shape[0]

    def halo_copy(i):
        return pltpu.make_async_remote_copy(
            src_ref=(k_ref, v_ref)[i].at[pl.ds(tokens - W, W)],
            dst_ref=halo.at[i],
            send_sem=halo_send.at[i],
            recv_sem=halo_recv.at[i],
            device_id={"seq": rank + 1},
            device_id_type=MESH,
        )

    def sum_copy(k):
        return pltpu.make_async_remote_copy(
            src_ref=local_sum,
            dst_ref=sums.at[k - 1],
            send_sem=sum_send.at[k - 1],
            recv_sem=sum_recv.at[k - 1],
            device_id={"seq": rank + k},
            device_id_type=MESH,
        )

    @pl.when(step == 0)
    def _():
        barrier = seq_barrier(rank, count)
        kf_ref[...] = nn(k_ref[...], key_map_ref[...]).astype(jnp.bfloat16)
        local_sum[...] = tn(kf_ref[...], v_ref[...])
        outer_mask[...] = head_masks(rows, heads, inner, hd)[0]
        v_ones[:, :hd] = v_ref[...]
        v_ones[:, hd:] = jnp.ones((tokens, hd), jnp.bfloat16)
        pl.semaphore_wait(barrier, count - 1)
        for k in range(1, count):
            @pl.when(rank + k < count)
            def _():
                sum_copy(k).start()
        @pl.when(rank + 1 < count)
        def _():
            halo_copy(0).start()
            halo_copy(1).start()

    outer = heads // inner
    maps = jnp.concatenate(
        [
            jnp.concatenate([maps_ref[(a * inner + b) * hd : (a * inner + b + 1) * hd] for b in range(inner)], 1)
            for a in range(outer)
        ], 0
    )
    inner_head = lax.broadcasted_iota(jnp.int32, (rows, hd), 0) % inner
    for start in range(0, q_ref.shape[0], rows):
        q = q_ref[start : start + rows, :]
        spread = nn(jnp.concatenate([q] * outer, 1) * outer_mask[...], maps)
        qf = spread[:, :hd]
        for b in range(1, inner):
            qf = jnp.where(inner_head == b, spread[:, b * hd : (b + 1) * hd], qf)
        qf_ref[start : start + rows, :] = qf.astype(jnp.bfloat16)

    tile_rows = TILE * heads
    tiles = late_q_ref.shape[0] // tile_rows
    for tile in range(tiles):
        first = pl.multiple_of((late_tile + step * tiles + tile) * TILE - W, TILE)
        k_win = k_ref[pl.ds(first, W + TILE), :]
        v_win = v_ones[pl.ds(first, W + TILE), :]
        for sub in range(0, tile_rows, rows):
            start = tile * tile_rows + sub
            late_soft_ref[start : start + rows, :] = window_softmax(
                late_q_ref[start : start + rows, :], k_win, v_win, ahead_of(rows, sub, heads)[1]
            )

    @pl.when(step == steps - 1)
    def _():
        prefix_ref[...] = jnp.zeros_like(prefix_ref)
        for k in range(1, count):
            @pl.when(rank + k < count)
            def _():
                sum_copy(k).wait_send()
            @pl.when(rank >= k)
            def _():
                sum_copy(k).wait_recv()
                prefix_ref[...] += sums[k - 1]
        @pl.when(rank + 1 < count)
        def _():
            halo_copy(0).wait_send()
            halo_copy(1).wait_send()
        @pl.when(rank >= 1)
        def _():
            halo_copy(0).wait_recv()
            halo_copy(1).wait_recv()
            rim_k_ref[...] = halo[0]
            rim_v_ref[...] = halo[1]
        @pl.when(rank == 0)
        def _():
            rim_k_ref[...] = jnp.zeros_like(rim_k_ref)
            rim_v_ref[...] = jnp.zeros_like(rim_v_ref)


def last_kernel(count, g_ref, g16_ref, out_ref, slots, send_sem, recv_sem):
    rank = lax.axis_index("seq")
    barrier = seq_barrier(rank, count)
    pl.semaphore_wait(barrier, count - 1)
    copies = []
    for k in range(1, count):
        target = lax.rem(rank + k, count)
        copies.append(pltpu.make_async_remote_copy(
            src_ref=g16_ref.at[target],
            dst_ref=slots.at[k - 1],
            send_sem=send_sem.at[k - 1],
            recv_sem=recv_sem.at[k - 1],
            device_id={"seq": target},
            device_id_type=MESH,
        ))
    for copy in copies:
        copy.start()
    total = g_ref[rank]
    for k, copy in enumerate(copies):
        copy.wait()
        total = total + slots[k].astype(jnp.float32)
    hd = out_ref.shape[2]
    for h in range(out_ref.shape[1]):
        out_ref[:, h, :] = total[:, h * hd : (h + 1) * hd]


def main_kernel(
    tokens_here, heads, inner, tiles, rows_sub, steps, early,
    q_ref, qf_ref, c_ref, late_soft_ref, k_ref, v_ref, kf_ref, rim_k_ref, rim_v_ref, prefix_ref,
    soft_ref, linear_ref, grad_ref, grad16_ref,
    k_ext, v_ext, outer_mask, inner_mask, state, grad,
):
    step = pl.program_id(0)
    rank = lax.axis_index("seq")
    hd = q_ref.shape[1]
    rows = TILE * heads
    outer = heads // inner

    @pl.when(step == 0)
    def _():
        k_ext[:W] = rim_k_ref[...]
        k_ext[W:] = k_ref[...]
        v_ext[:W, :hd] = rim_v_ref[...]
        v_ext[W:, :hd] = v_ref[...]
        v_ext[:, hd:] = jnp.ones((v_ext.shape[0], hd), jnp.bfloat16)
        outer_mask[...], inner_mask[...] = head_masks(rows_sub, heads, inner, hd)
        state[...] = prefix_ref[...]
        grad[...] = jnp.zeros_like(grad)

    zero = jnp.zeros((TILE, hd), jnp.bfloat16)
    mids = W // TILE

    def block(with_softmax):
        for tile in range(tiles):
            index = step * tiles + tile
            first = pl.multiple_of(index * TILE, TILE)
            k_win = k_ext[pl.ds(first, W + TILE), :]
            v_win = v_ext[pl.ds(first, W + TILE), :]
            kf = kf_ref[pl.ds(first, TILE), :]
            v = v_ref[pl.ds(first, TILE), :]
            s_now = state[...]

            def diagonal(a, b):
                return jnp.concatenate(
                    [jnp.concatenate([a, zero], 1), jnp.concatenate([zero, b], 1)], 0
                )

            into_scores = diagonal(kf, v)
            carried = diagonal(s_now.astype(jnp.bfloat16), s_now.T.astype(jnp.bfloat16))
            from_scores = jnp.concatenate([diagonal(v, kf), carried], 0)
            invalid = [
                jnp.where((rank == 0) & (index + j < mids), -1e30, 0.0).astype(jnp.float32)
                for j in range(mids)
            ]
            queries, gradients = [], []
            for sub in range(rows // rows_sub):
                start = tile * rows + sub * rows_sub
                q = q_ref[start : start + rows_sub, :]
                c = c_ref[start : start + rows_sub, :]
                local, ahead = ahead_of(rows_sub, sub * rows_sub, heads)
                if with_softmax:
                    soft_ref[start : start + rows_sub, :] = window_softmax(q, k_win, v_win, ahead, invalid)
                pair = jnp.concatenate([qf_ref[start : start + rows_sub, :], c], 1)
                pair_scores = nt(pair, into_scores)
                ahead_two = jnp.concatenate([ahead, ahead], 1)
                pair_scores = jnp.where(ahead_two, 0.0, pair_scores).astype(jnp.bfloat16)
                pair_out = nn(jnp.concatenate([pair_scores, pair], 1), from_scores)
                position = rank * tokens_here + index * TILE + local + 1
                factor = lax.rsqrt(position.astype(jnp.float32))
                linear_ref[start : start + rows_sub, :] = (factor * pair_out[:, :hd]).astype(jnp.bfloat16)
                fg = (factor * pair_out[:, hd:]).astype(jnp.bfloat16)
                queries.append(jnp.concatenate([q] * outer, 1) * outer_mask[...])
                gradients.append(jnp.concatenate([fg] * inner, 1) * inner_mask[...])
            grad[...] += tn(jnp.concatenate(queries, 0), jnp.concatenate(gradients, 0))
            state[...] = s_now + tn(kf, v)

    @pl.when(step < early)
    def _():
        block(True)

    @pl.when(step >= early)
    def _():
        soft_ref[...] = late_soft_ref[...]
        block(False)

    @pl.when(step == steps - 1)
    def _():
        for a in range(outer):
            block = grad[a * hd : (a + 1) * hd, :]
            block = block.reshape(grad_ref.shape[:2] + (inner * hd,))
            grad_ref[:, :, a * inner * hd : (a + 1) * inner * hd] = block
            grad16_ref[:, :, a * inner * hd : (a + 1) * inner * hd] = block.astype(jnp.bfloat16)


def per_device(queries, keys, values, query_maps, key_map, linear_cotangent):
    tokens_here, hd = keys.shape
    heads = queries.shape[1]
    count = lax.axis_size("seq")
    inner = 2 if heads % 2 == 0 else 1
    outer = heads // inner
    share = hd // count
    tiles = 4
    rows_sub = min(256, TILE * heads)
    step_rows = TILE * tiles * heads
    total = tokens_here * heads
    steps = total // step_rows
    early = steps // 2
    late_rows = (steps - early) * step_rows // steps
    whole = lambda a: pl.BlockSpec(a.shape, lambda i: (0,) * len(a.shape))
    rows_spec = pl.BlockSpec((step_rows, hd), lambda i: (i, 0))
    maps = query_maps.reshape(heads * hd, hd)
    queries = queries.reshape(total, hd)
    cotangent = linear_cotangent.reshape(total, hd)

    rows16 = jax.ShapeDtypeStruct((total, hd), jnp.bfloat16)
    late16 = jax.ShapeDtypeStruct((steps * late_rows, hd), jnp.bfloat16)
    kf16 = jax.ShapeDtypeStruct((tokens_here, hd), jnp.bfloat16)
    rim = jax.ShapeDtypeStruct((W, hd), jnp.bfloat16)
    square = jax.ShapeDtypeStruct((hd, hd), jnp.float32)
    dma = pltpu.SemaphoreType.DMA
    query_features, late_soft, key_features, rim_keys, rim_values, prefix = pl.pallas_call(
        functools.partial(first_kernel, count, heads, inner, steps, early * tiles),
        grid=(steps,),
        in_specs=[rows_spec, pl.BlockSpec((late_rows, hd), lambda i: (i + early * step_rows // late_rows, 0))]
        + [whole(a) for a in (maps, keys, values, key_map)],
        out_specs=[rows_spec, pl.BlockSpec((late_rows, hd), lambda i: (i, 0))]
        + [whole(a) for a in (kf16, rim, rim, square)],
        out_shape=[rows16, late16, kf16, rim, rim, square],
        scratch_shapes=[
            pltpu.VMEM((tokens_here, 2 * hd), jnp.bfloat16),
            pltpu.VMEM((rows_sub, outer * hd), jnp.bfloat16),
            pltpu.VMEM((hd, hd), jnp.float32),
            pltpu.VMEM((count - 1, hd, hd), jnp.float32),
            pltpu.VMEM((2, W, hd), jnp.bfloat16),
            dma((count - 1,)), dma((count - 1,)), dma((2,)), dma((2,)),
        ],
        compiler_params=pltpu.CompilerParams(
            dimension_semantics=("arbitrary",), collective_id=0, has_side_effects=True
        ),
        name="features",
    )(queries, queries, maps, keys, values, key_map)

    pieces = (count, share, heads * hd)
    small = (keys, values, key_features, rim_keys, rim_values, prefix)
    soft, linear, grad, grad16 = pl.pallas_call(
        functools.partial(main_kernel, tokens_here, heads, inner, tiles, rows_sub, steps, early),
        grid=(steps,),
        in_specs=[rows_spec] * 3
        + [pl.BlockSpec((step_rows, hd), lambda i: (jnp.maximum(i - early, 0), 0))]
        + [whole(a) for a in small],
        out_specs=[rows_spec] * 2 + [pl.BlockSpec(pieces, lambda i: (0, 0, 0))] * 2,
        out_shape=[
            rows16, rows16,
            jax.ShapeDtypeStruct(pieces, jnp.float32),
            jax.ShapeDtypeStruct(pieces, jnp.bfloat16),
        ],
        scratch_shapes=[
            pltpu.VMEM((tokens_here + W, hd), jnp.bfloat16),
            pltpu.VMEM((tokens_here + W, 2 * hd), jnp.bfloat16),
            pltpu.VMEM((rows_sub, outer * hd), jnp.bfloat16),
            pltpu.VMEM((rows_sub, inner * hd), jnp.bfloat16),
            pltpu.VMEM((hd, hd), jnp.float32),
            pltpu.VMEM((outer * hd, inner * hd), jnp.float32),
        ],
        compiler_params=pltpu.CompilerParams(dimension_semantics=("arbitrary",)),
        name="attention",
    )(queries, query_features, cotangent, late_soft, *small)

    vmem = pl.BlockSpec(memory_space=pltpu.VMEM)
    mine = pl.pallas_call(
        functools.partial(last_kernel, count),
        in_specs=[vmem, vmem],
        out_specs=vmem,
        out_shape=jax.ShapeDtypeStruct((share, heads, hd), jnp.float32),
        scratch_shapes=[
            pltpu.VMEM((count - 1,) + pieces[1:], jnp.bfloat16), dma((count - 1,)), dma((count - 1,)),
        ],
        compiler_params=pltpu.CompilerParams(collective_id=1, has_side_effects=True),
        name="map_gradient",
    )(grad, grad16)
    shape = (tokens_here, heads, hd)
    return soft.reshape(shape), linear.reshape(shape), mine


def solution(mesh):
    rows = P(("groups", "seq"), ("head", "rep"), None)
    return jax.shard_map(
        per_device,
        mesh=mesh,
        in_specs=(
            rows,
            P(("groups", "seq"), None),
            P(("groups", "seq"), None),
            P(("groups", "head", "rep"), None, None),
            P("groups", None),
            rows,
        ),
        out_specs=(rows, rows, rows),
        check_vma=False,
    )
```

```python
import functools

import jax
import jax.numpy as jnp
from jax import lax
from jax.experimental import pallas as pl
from jax.experimental.pallas import tpu as pltpu
from jax.sharding import PartitionSpec as P

W = 512
TILE = 128
MESH = pl.DeviceIdType.MESH


def nt(a, b):
    return lax.dot_general(a, b, (((1,), (1,)), ((), ())), preferred_element_type=jnp.float32)


def tn(a, b):
    return lax.dot_general(a, b, (((0,), (0,)), ((), ())), preferred_element_type=jnp.float32)


def nn(a, b):
    return jnp.dot(a, b, preferred_element_type=jnp.float32)


def head_masks(rows, heads, inner, hd):
    def mask(parts, of_head):
        shape = (rows, parts * hd)
        head = lax.broadcasted_iota(jnp.int32, shape, 0) % heads
        part = lax.broadcasted_iota(jnp.int32, shape, 1) // hd
        return jnp.where(of_head(head) == part, 1.0, 0.0).astype(jnp.bfloat16)

    return mask(heads // inner, lambda h: h // inner), mask(inner, lambda h: h % inner)


def ahead_of(rows, start, heads):
    shape = (rows, TILE)
    local = (lax.broadcasted_iota(jnp.int32, shape, 0) + start) // heads
    return local, lax.broadcasted_iota(jnp.int32, shape, 1) > local


def window_softmax(q, k_win, v_win, ahead, invalid=None):
    hd = q.shape[1]
    mids = W // TILE
    scale = hd ** (-0.5) * 1.4426950408889634
    scores = nt(q, k_win)
    parts = [scores[:, j * TILE : (j + 1) * TILE] for j in range(mids + 1)]
    if invalid is not None:
        parts = [p + invalid[j] if j < mids else p for j, p in enumerate(parts)]
    kept = [jnp.where(ahead, parts[0], parts[mids])] + parts[1:mids]
    highest = jnp.max(functools.reduce(jnp.maximum, kept), axis=1, keepdims=True)
    kept = [jnp.exp2((p - highest) * scale) for p in kept]
    weights = jnp.concatenate(
        [jnp.where(ahead, kept[0], 0.0).astype(jnp.bfloat16)]
        + [p.astype(jnp.bfloat16) for p in kept[1:]]
        + [jnp.where(ahead, 0.0, kept[0]).astype(jnp.bfloat16)], 1
    )
    soft = nn(weights, v_win)
    return (soft[:, :hd] / soft[:, hd:]).astype(jnp.bfloat16)


def seq_barrier(rank, count):
    barrier = pltpu.get_barrier_semaphore()
    for k in range(1, count):
        pl.semaphore_signal(
            barrier, inc=1, device_id={"seq": lax.rem(rank + k, count)}, device_id_type=MESH
        )
    return barrier


def first_kernel(
    count, heads, inner, steps, late_tile,
    q_ref, late_q_ref, maps_ref, k_ref, v_ref, key_map_ref,
    qf_ref, late_soft_ref, kf_ref, rim_k_ref, rim_v_ref, prefix_ref,
    v_ones, outer_mask, local_sum, sums, halo, sum_send, sum_recv, halo_send, halo_recv,
):
    step = pl.program_id(0)
    rank = lax.axis_index("seq")
    tokens, hd = k_ref.shape
    rows = outer_mask.shape[0]

    def halo_copy(i):
        return pltpu.make_async_remote_copy(
            src_ref=(k_ref, v_ref)[i].at[pl.ds(tokens - W, W)],
            dst_ref=halo.at[i],
            send_sem=halo_send.at[i],
            recv_sem=halo_recv.at[i],
            device_id={"seq": rank + 1},
            device_id_type=MESH,
        )

    def sum_copy(k):
        return pltpu.make_async_remote_copy(
            src_ref=local_sum,
            dst_ref=sums.at[k - 1],
            send_sem=sum_send.at[k - 1],
            recv_sem=sum_recv.at[k - 1],
            device_id={"seq": rank + k},
            device_id_type=MESH,
        )

    @pl.when(step == 0)
    def _():
        barrier = seq_barrier(rank, count)
        kf_ref[...] = nn(k_ref[...], key_map_ref[...]).astype(jnp.bfloat16)
        local_sum[...] = tn(kf_ref[...], v_ref[...])
        outer_mask[...] = head_masks(rows, heads, inner, hd)[0]
        v_ones[:, :hd] = v_ref[...]
        v_ones[:, hd:] = jnp.ones((tokens, hd), jnp.bfloat16)
        pl.semaphore_wait(barrier, count - 1)
        for k in range(1, count):
            @pl.when(rank + k < count)
            def _():
                sum_copy(k).start()
        @pl.when(rank + 1 < count)
        def _():
            halo_copy(0).start()
            halo_copy(1).start()

    outer = heads // inner
    maps = jnp.concatenate(
        [
            jnp.concatenate([maps_ref[(a * inner + b) * hd : (a * inner + b + 1) * hd] for b in range(inner)], 1)
            for a in range(outer)
        ], 0
    )
    inner_head = lax.broadcasted_iota(jnp.int32, (rows, hd), 0) % inner
    for start in range(0, q_ref.shape[0], rows):
        q = q_ref[start : start + rows, :]
        spread = nn(jnp.concatenate([q] * outer, 1) * outer_mask[...], maps)
        qf = spread[:, :hd]
        for b in range(1, inner):
            qf = jnp.where(inner_head == b, spread[:, b * hd : (b + 1) * hd], qf)
        qf_ref[start : start + rows, :] = qf.astype(jnp.bfloat16)

    tile_rows = TILE * heads
    tiles = late_q_ref.shape[0] // tile_rows
    for tile in range(tiles):
        first = pl.multiple_of((late_tile + step * tiles + tile) * TILE - W, TILE)
        k_win = k_ref[pl.ds(first, W + TILE), :]
        v_win = v_ones[pl.ds(first, W + TILE), :]
        for sub in range(0, tile_rows, rows):
            start = tile * tile_rows + sub
            late_soft_ref[start : start + rows, :] = window_softmax(
                late_q_ref[start : start + rows, :], k_win, v_win, ahead_of(rows, sub, heads)[1]
            )

    @pl.when(step == steps - 1)
    def _():
        prefix_ref[...] = jnp.zeros_like(prefix_ref)
        for k in range(1, count):
            @pl.when(rank + k < count)
            def _():
                sum_copy(k).wait_send()
            @pl.when(rank >= k)
            def _():
                sum_copy(k).wait_recv()
                prefix_ref[...] += sums[k - 1]
        @pl.when(rank + 1 < count)
        def _():
            halo_copy(0).wait_send()
            halo_copy(1).wait_send()
        @pl.when(rank >= 1)
        def _():
            halo_copy(0).wait_recv()
            halo_copy(1).wait_recv()
            rim_k_ref[...] = halo[0]
            rim_v_ref[...] = halo[1]
        @pl.when(rank == 0)
        def _():
            rim_k_ref[...] = jnp.zeros_like(rim_k_ref)
            rim_v_ref[...] = jnp.zeros_like(rim_v_ref)


def last_kernel(count, g_ref, g16_ref, out_ref, slots, send_sem, recv_sem):
    rank = lax.axis_index("seq")
    barrier = seq_barrier(rank, count)
    pl.semaphore_wait(barrier, count - 1)
    copies = []
    for k in range(1, count):
        target = lax.rem(rank + k, count)
        copies.append(pltpu.make_async_remote_copy(
            src_ref=g16_ref.at[target],
            dst_ref=slots.at[k - 1],
            send_sem=send_sem.at[k - 1],
            recv_sem=recv_sem.at[k - 1],
            device_id={"seq": target},
            device_id_type=MESH,
        ))
    for copy in copies:
        copy.start()
    total = g_ref[rank]
    for k, copy in enumerate(copies):
        copy.wait()
        total = total + slots[k].astype(jnp.float32)
    hd = out_ref.shape[2]
    for h in range(out_ref.shape[1]):
        out_ref[:, h, :] = total[:, h * hd : (h + 1) * hd]


def main_kernel(
    tokens_here, heads, inner, tiles, rows_sub, steps, early,
    q_ref, qf_ref, c_ref, late_soft_ref, k_ref, v_ref, kf_ref, rim_k_ref, rim_v_ref, prefix_ref,
    soft_ref, linear_ref, grad_ref, grad16_ref,
    k_ext, v_ext, outer_mask, inner_mask, state, grad,
):
    step = pl.program_id(0)
    rank = lax.axis_index("seq")
    hd = q_ref.shape[1]
    rows = TILE * heads
    outer = heads // inner

    @pl.when(step == 0)
    def _():
        k_ext[:W] = rim_k_ref[...]
        k_ext[W:] = k_ref[...]
        v_ext[:W, :hd] = rim_v_ref[...]
        v_ext[W:, :hd] = v_ref[...]
        v_ext[:, hd:] = jnp.ones((v_ext.shape[0], hd), jnp.bfloat16)
        outer_mask[...], inner_mask[...] = head_masks(rows_sub, heads, inner, hd)
        state[...] = prefix_ref[...]
        grad[...] = jnp.zeros_like(grad)

    zero = jnp.zeros((TILE, hd), jnp.bfloat16)
    mids = W // TILE

    def block(with_softmax):
        for tile in range(tiles):
            index = step * tiles + tile
            first = pl.multiple_of(index * TILE, TILE)
            k_win = k_ext[pl.ds(first, W + TILE), :]
            v_win = v_ext[pl.ds(first, W + TILE), :]
            kf = kf_ref[pl.ds(first, TILE), :]
            v = v_ref[pl.ds(first, TILE), :]
            s_now = state[...]

            def diagonal(a, b):
                return jnp.concatenate(
                    [jnp.concatenate([a, zero], 1), jnp.concatenate([zero, b], 1)], 0
                )

            into_scores = diagonal(kf, v)
            carried = diagonal(s_now.astype(jnp.bfloat16), s_now.T.astype(jnp.bfloat16))
            from_scores = jnp.concatenate([diagonal(v, kf), carried], 0)
            invalid = [
                jnp.where((rank == 0) & (index + j < mids), -1e30, 0.0).astype(jnp.float32)
                for j in range(mids)
            ]
            queries, gradients = [], []
            for sub in range(rows // rows_sub):
                start = tile * rows + sub * rows_sub
                q = q_ref[start : start + rows_sub, :]
                c = c_ref[start : start + rows_sub, :]
                local, ahead = ahead_of(rows_sub, sub * rows_sub, heads)
                if with_softmax:
                    soft_ref[start : start + rows_sub, :] = window_softmax(q, k_win, v_win, ahead, invalid)
                pair = jnp.concatenate([qf_ref[start : start + rows_sub, :], c], 1)
                pair_scores = nt(pair, into_scores)
                ahead_two = jnp.concatenate([ahead, ahead], 1)
                pair_scores = jnp.where(ahead_two, 0.0, pair_scores).astype(jnp.bfloat16)
                pair_out = nn(jnp.concatenate([pair_scores, pair], 1), from_scores)
                position = rank * tokens_here + index * TILE + local + 1
                factor = lax.rsqrt(position.astype(jnp.float32))
                linear_ref[start : start + rows_sub, :] = (factor * pair_out[:, :hd]).astype(jnp.bfloat16)
                fg = (factor * pair_out[:, hd:]).astype(jnp.bfloat16)
                queries.append(jnp.concatenate([q] * outer, 1) * outer_mask[...])
                gradients.append(jnp.concatenate([fg] * inner, 1) * inner_mask[...])
            grad[...] += tn(jnp.concatenate(queries, 0), jnp.concatenate(gradients, 0))
            state[...] = s_now + tn(kf, v)

    @pl.when(step < early)
    def _():
        block(True)

    @pl.when(step >= early)
    def _():
        soft_ref[...] = late_soft_ref[...]
        block(False)

    @pl.when(step == steps - 1)
    def _():
        for a in range(outer):
            block = grad[a * hd : (a + 1) * hd, :]
            block = block.reshape(grad_ref.shape[:2] + (inner * hd,))
            grad_ref[:, :, a * inner * hd : (a + 1) * inner * hd] = block
            grad16_ref[:, :, a * inner * hd : (a + 1) * inner * hd] = block.astype(jnp.bfloat16)


def per_device(queries, keys, values, query_maps, key_map, linear_cotangent):
    tokens_here, hd = keys.shape
    heads = queries.shape[1]
    count = lax.axis_size("seq")
    inner = 2 if heads % 2 == 0 else 1
    outer = heads // inner
    share = hd // count
    tiles = 4
    rows_sub = min(512, TILE * heads)
    step_rows = TILE * tiles * heads
    total = tokens_here * heads
    steps = total // step_rows
    early = steps // 2
    late_rows = (steps - early) * step_rows // steps
    whole = lambda a: pl.BlockSpec(a.shape, lambda i: (0,) * len(a.shape))
    rows_spec = pl.BlockSpec((step_rows, hd), lambda i: (i, 0))
    maps = query_maps.reshape(heads * hd, hd)
    queries = queries.reshape(total, hd)
    cotangent = linear_cotangent.reshape(total, hd)

    rows16 = jax.ShapeDtypeStruct((total, hd), jnp.bfloat16)
    late16 = jax.ShapeDtypeStruct((steps * late_rows, hd), jnp.bfloat16)
    kf16 = jax.ShapeDtypeStruct((tokens_here, hd), jnp.bfloat16)
    rim = jax.ShapeDtypeStruct((W, hd), jnp.bfloat16)
    square = jax.ShapeDtypeStruct((hd, hd), jnp.float32)
    dma = pltpu.SemaphoreType.DMA
    query_features, late_soft, key_features, rim_keys, rim_values, prefix = pl.pallas_call(
        functools.partial(first_kernel, count, heads, inner, steps, early * tiles),
        grid=(steps,),
        in_specs=[rows_spec, pl.BlockSpec((late_rows, hd), lambda i: (i + early * step_rows // late_rows, 0))]
        + [whole(a) for a in (maps, keys, values, key_map)],
        out_specs=[rows_spec, pl.BlockSpec((late_rows, hd), lambda i: (i, 0))]
        + [whole(a) for a in (kf16, rim, rim, square)],
        out_shape=[rows16, late16, kf16, rim, rim, square],
        scratch_shapes=[
            pltpu.VMEM((tokens_here, 2 * hd), jnp.bfloat16),
            pltpu.VMEM((rows_sub, outer * hd), jnp.bfloat16),
            pltpu.VMEM((hd, hd), jnp.float32),
            pltpu.VMEM((count - 1, hd, hd), jnp.float32),
            pltpu.VMEM((2, W, hd), jnp.bfloat16),
            dma((count - 1,)), dma((count - 1,)), dma((2,)), dma((2,)),
        ],
        compiler_params=pltpu.CompilerParams(
            dimension_semantics=("arbitrary",), collective_id=0, has_side_effects=True
        ),
        name="features",
    )(queries, queries, maps, keys, values, key_map)

    pieces = (count, share, heads * hd)
    small = (keys, values, key_features, rim_keys, rim_values, prefix)
    soft, linear, grad, grad16 = pl.pallas_call(
        functools.partial(main_kernel, tokens_here, heads, inner, tiles, rows_sub, steps, early),
        grid=(steps,),
        in_specs=[rows_spec] * 3
        + [pl.BlockSpec((step_rows, hd), lambda i: (jnp.maximum(i - early, 0), 0))]
        + [whole(a) for a in small],
        out_specs=[rows_spec] * 2 + [pl.BlockSpec(pieces, lambda i: (0, 0, 0))] * 2,
        out_shape=[
            rows16, rows16,
            jax.ShapeDtypeStruct(pieces, jnp.float32),
            jax.ShapeDtypeStruct(pieces, jnp.bfloat16),
        ],
        scratch_shapes=[
            pltpu.VMEM((tokens_here + W, hd), jnp.bfloat16),
            pltpu.VMEM((tokens_here + W, 2 * hd), jnp.bfloat16),
            pltpu.VMEM((rows_sub, outer * hd), jnp.bfloat16),
            pltpu.VMEM((rows_sub, inner * hd), jnp.bfloat16),
            pltpu.VMEM((hd, hd), jnp.float32),
            pltpu.VMEM((outer * hd, inner * hd), jnp.float32),
        ],
        compiler_params=pltpu.CompilerParams(dimension_semantics=("arbitrary",)),
        name="attention",
    )(queries, query_features, cotangent, late_soft, *small)

    vmem = pl.BlockSpec(memory_space=pltpu.VMEM)
    mine = pl.pallas_call(
        functools.partial(last_kernel, count),
        in_specs=[vmem, vmem],
        out_specs=vmem,
        out_shape=jax.ShapeDtypeStruct((share, heads, hd), jnp.float32),
        scratch_shapes=[
            pltpu.VMEM((count - 1,) + pieces[1:], jnp.bfloat16), dma((count - 1,)), dma((count - 1,)),
        ],
        compiler_params=pltpu.CompilerParams(collective_id=1, has_side_effects=True),
        name="map_gradient",
    )(grad, grad16)
    shape = (tokens_here, heads, hd)
    return soft.reshape(shape), linear.reshape(shape), mine


def solution(mesh):
    rows = P(("groups", "seq"), ("head", "rep"), None)
    return jax.shard_map(
        per_device,
        mesh=mesh,
        in_specs=(
            rows,
            P(("groups", "seq"), None),
            P(("groups", "seq"), None),
            P(("groups", "head", "rep"), None, None),
            P("groups", None),
            rows,
        ),
        out_specs=(rows, rows, rows),
        check_vma=False,
    )
```

```python
import functools

import jax
import jax.numpy as jnp
from jax import lax
from jax.experimental import pallas as pl
from jax.experimental.pallas import tpu as pltpu
from jax.sharding import PartitionSpec as P

W = 512
TILE = 128
MESH = pl.DeviceIdType.MESH


def nt(a, b):
    return lax.dot_general(a, b, (((1,), (1,)), ((), ())), preferred_element_type=jnp.float32)


def tn(a, b):
    return lax.dot_general(a, b, (((0,), (0,)), ((), ())), preferred_element_type=jnp.float32)


def nn(a, b):
    return jnp.dot(a, b, preferred_element_type=jnp.float32)


def head_masks(rows, heads, inner, hd):
    def mask(parts, of_head):
        shape = (rows, parts * hd)
        head = lax.broadcasted_iota(jnp.int32, shape, 0) % heads
        part = lax.broadcasted_iota(jnp.int32, shape, 1) // hd
        return jnp.where(of_head(head) == part, 1.0, 0.0).astype(jnp.bfloat16)

    return mask(heads // inner, lambda h: h // inner), mask(inner, lambda h: h % inner)


def ahead_of(rows, start, heads):
    shape = (rows, TILE)
    local = (lax.broadcasted_iota(jnp.int32, shape, 0) + start) // heads
    return local, lax.broadcasted_iota(jnp.int32, shape, 1) > local


def window_softmax(q, k_win, v_win, ahead, invalid=None):
    hd = q.shape[1]
    mids = W // TILE
    scale = hd ** (-0.5) * 1.4426950408889634
    scores = nt(q, k_win)
    parts = [scores[:, j * TILE : (j + 1) * TILE] for j in range(mids + 1)]
    if invalid is not None:
        parts = [p + invalid[j] if j < mids else p for j, p in enumerate(parts)]
    kept = [jnp.where(ahead, parts[0], parts[mids])] + parts[1:mids]
    highest = jnp.max(functools.reduce(jnp.maximum, kept), axis=1, keepdims=True)
    kept = [jnp.exp2((p - highest) * scale) for p in kept]
    weights = jnp.concatenate(
        [jnp.where(ahead, kept[0], 0.0).astype(jnp.bfloat16)]
        + [p.astype(jnp.bfloat16) for p in kept[1:]]
        + [jnp.where(ahead, 0.0, kept[0]).astype(jnp.bfloat16)], 1
    )
    soft = nn(weights, v_win)
    return (soft[:, :hd] / soft[:, hd:]).astype(jnp.bfloat16)


def seq_barrier(rank, count):
    barrier = pltpu.get_barrier_semaphore()
    for k in range(1, count):
        pl.semaphore_signal(
            barrier, inc=1, device_id={"seq": lax.rem(rank + k, count)}, device_id_type=MESH
        )
    return barrier


def first_kernel(
    count, heads, inner, steps, late_tile, tiles, q_ref, *refs,
):
    late_q_refs, refs = refs[:tiles], refs[tiles:]
    (
    maps_ref, k_ref, v_ref, key_map_ref,
    qf_ref, late_soft_ref, kf_ref, rim_k_ref, rim_v_ref, prefix_ref,
    v_ones, outer_mask, local_sum, sums, halo, sum_send, sum_recv, halo_send, halo_recv,
    ) = refs
    step = pl.program_id(0)
    rank = lax.axis_index("seq")
    tokens, hd = k_ref.shape
    rows = outer_mask.shape[0]

    def halo_copy(i):
        return pltpu.make_async_remote_copy(
            src_ref=(k_ref, v_ref)[i].at[pl.ds(tokens - W, W)],
            dst_ref=halo.at[i],
            send_sem=halo_send.at[i],
            recv_sem=halo_recv.at[i],
            device_id={"seq": rank + 1},
            device_id_type=MESH,
        )

    def sum_copy(k):
        return pltpu.make_async_remote_copy(
            src_ref=local_sum,
            dst_ref=sums.at[k - 1],
            send_sem=sum_send.at[k - 1],
            recv_sem=sum_recv.at[k - 1],
            device_id={"seq": rank + k},
            device_id_type=MESH,
        )

    @pl.when(step == 0)
    def _():
        barrier = seq_barrier(rank, count)
        kf_ref[...] = nn(k_ref[...], key_map_ref[...]).astype(jnp.bfloat16)
        local_sum[...] = tn(kf_ref[...], v_ref[...])
        outer_mask[...] = head_masks(rows, heads, inner, hd)[0]
        v_ones[:, :hd] = v_ref[...]
        v_ones[:, hd:] = jnp.ones((tokens, hd), jnp.bfloat16)
        pl.semaphore_wait(barrier, count - 1)
        for k in range(1, count):
            @pl.when(rank + k < count)
            def _():
                sum_copy(k).start()
        @pl.when(rank + 1 < count)
        def _():
            halo_copy(0).start()
            halo_copy(1).start()

    outer = heads // inner
    maps = jnp.concatenate(
        [
            jnp.concatenate([maps_ref[(a * inner + b) * hd : (a * inner + b + 1) * hd] for b in range(inner)], 1)
            for a in range(outer)
        ], 0
    )
    inner_head = lax.broadcasted_iota(jnp.int32, (rows, hd), 0) % inner
    for start in range(0, q_ref.shape[0], rows):
        q = q_ref[start : start + rows, :]
        spread = nn(jnp.concatenate([q] * outer, 1) * outer_mask[...], maps)
        qf = spread[:, :hd]
        for b in range(1, inner):
            qf = jnp.where(inner_head == b, spread[:, b * hd : (b + 1) * hd], qf)
        qf_ref[start : start + rows, :] = qf.astype(jnp.bfloat16)

    tile_rows = TILE * heads
    for tile in range(tiles):
        first = pl.multiple_of((late_tile + step * tiles + tile) * TILE - W, TILE)
        k_win = k_ref[pl.ds(first, W + TILE), :]
        v_win = v_ones[pl.ds(first, W + TILE), :]
        for sub in range(0, tile_rows, rows):
            start = tile * tile_rows + sub
            late_soft_ref[start : start + rows, :] = window_softmax(
                late_q_refs[tile][sub : sub + rows, :], k_win, v_win, ahead_of(rows, sub, heads)[1]
            )

    @pl.when(step == steps - 1)
    def _():
        prefix_ref[...] = jnp.zeros_like(prefix_ref)
        for k in range(1, count):
            @pl.when(rank + k < count)
            def _():
                sum_copy(k).wait_send()
            @pl.when(rank >= k)
            def _():
                sum_copy(k).wait_recv()
                prefix_ref[...] += sums[k - 1]
        @pl.when(rank + 1 < count)
        def _():
            halo_copy(0).wait_send()
            halo_copy(1).wait_send()
        @pl.when(rank >= 1)
        def _():
            halo_copy(0).wait_recv()
            halo_copy(1).wait_recv()
            rim_k_ref[...] = halo[0]
            rim_v_ref[...] = halo[1]
        @pl.when(rank == 0)
        def _():
            rim_k_ref[...] = jnp.zeros_like(rim_k_ref)
            rim_v_ref[...] = jnp.zeros_like(rim_v_ref)


def last_kernel(count, g_ref, g16_ref, out_ref, slots, send_sem, recv_sem):
    rank = lax.axis_index("seq")
    barrier = seq_barrier(rank, count)
    pl.semaphore_wait(barrier, count - 1)
    copies = []
    for k in range(1, count):
        target = lax.rem(rank + k, count)
        copies.append(pltpu.make_async_remote_copy(
            src_ref=g16_ref.at[target],
            dst_ref=slots.at[k - 1],
            send_sem=send_sem.at[k - 1],
            recv_sem=recv_sem.at[k - 1],
            device_id={"seq": target},
            device_id_type=MESH,
        ))
    for copy in copies:
        copy.start()
    total = g_ref[rank]
    for k, copy in enumerate(copies):
        copy.wait()
        total = total + slots[k].astype(jnp.float32)
    hd = out_ref.shape[2]
    for h in range(out_ref.shape[1]):
        out_ref[:, h, :] = total[:, h * hd : (h + 1) * hd]


def main_kernel(
    tokens_here, heads, inner, tiles, rows_sub, steps, early,
    q_ref, qf_ref, c_ref, late_soft_ref, k_ref, v_ref, kf_ref, rim_k_ref, rim_v_ref, prefix_ref,
    soft_ref, linear_ref, grad_ref, grad16_ref,
    k_ext, v_ext, outer_mask, inner_mask, state, grad,
):
    step = pl.program_id(0)
    rank = lax.axis_index("seq")
    hd = q_ref.shape[1]
    rows = TILE * heads
    outer = heads // inner

    @pl.when(step == 0)
    def _():
        k_ext[:W] = rim_k_ref[...]
        k_ext[W:] = k_ref[...]
        v_ext[:W, :hd] = rim_v_ref[...]
        v_ext[W:, :hd] = v_ref[...]
        v_ext[:, hd:] = jnp.ones((v_ext.shape[0], hd), jnp.bfloat16)
        outer_mask[...], inner_mask[...] = head_masks(rows_sub, heads, inner, hd)
        state[...] = prefix_ref[...]
        grad[...] = jnp.zeros_like(grad)

    zero = jnp.zeros((TILE, hd), jnp.bfloat16)
    mids = W // TILE

    def block(with_softmax):
        for tile in range(tiles):
            index = step * tiles + tile
            first = pl.multiple_of(index * TILE, TILE)
            k_win = k_ext[pl.ds(first, W + TILE), :]
            v_win = v_ext[pl.ds(first, W + TILE), :]
            kf = kf_ref[pl.ds(first, TILE), :]
            v = v_ref[pl.ds(first, TILE), :]
            s_now = state[...]

            def diagonal(a, b):
                return jnp.concatenate(
                    [jnp.concatenate([a, zero], 1), jnp.concatenate([zero, b], 1)], 0
                )

            into_scores = diagonal(kf, v)
            carried = diagonal(s_now.astype(jnp.bfloat16), s_now.T.astype(jnp.bfloat16))
            from_scores = jnp.concatenate([diagonal(v, kf), carried], 0)
            invalid = [
                jnp.where((rank == 0) & (index + j < mids), -1e30, 0.0).astype(jnp.float32)
                for j in range(mids)
            ]
            queries, gradients = [], []
            for sub in range(rows // rows_sub):
                start = tile * rows + sub * rows_sub
                q = q_ref[start : start + rows_sub, :]
                c = c_ref[start : start + rows_sub, :]
                local, ahead = ahead_of(rows_sub, sub * rows_sub, heads)
                if with_softmax:
                    soft_ref[start : start + rows_sub, :] = window_softmax(q, k_win, v_win, ahead, invalid)
                pair = jnp.concatenate([qf_ref[start : start + rows_sub, :], c], 1)
                pair_scores = nt(pair, into_scores)
                ahead_two = jnp.concatenate([ahead, ahead], 1)
                pair_scores = jnp.where(ahead_two, 0.0, pair_scores).astype(jnp.bfloat16)
                pair_out = nn(jnp.concatenate([pair_scores, pair], 1), from_scores)
                position = rank * tokens_here + index * TILE + local + 1
                factor = lax.rsqrt(position.astype(jnp.float32))
                linear_ref[start : start + rows_sub, :] = (factor * pair_out[:, :hd]).astype(jnp.bfloat16)
                fg = (factor * pair_out[:, hd:]).astype(jnp.bfloat16)
                queries.append(jnp.concatenate([q] * outer, 1) * outer_mask[...])
                gradients.append(jnp.concatenate([fg] * inner, 1) * inner_mask[...])
            grad[...] += tn(jnp.concatenate(queries, 0), jnp.concatenate(gradients, 0))
            state[...] = s_now + tn(kf, v)

    @pl.when(step < early)
    def _():
        block(True)

    @pl.when(step >= early)
    def _():
        soft_ref[...] = late_soft_ref[...]
        block(False)

    @pl.when(step == steps - 1)
    def _():
        for a in range(outer):
            block = grad[a * hd : (a + 1) * hd, :]
            block = block.reshape(grad_ref.shape[:2] + (inner * hd,))
            grad_ref[:, :, a * inner * hd : (a + 1) * inner * hd] = block
            grad16_ref[:, :, a * inner * hd : (a + 1) * inner * hd] = block.astype(jnp.bfloat16)


def per_device(queries, keys, values, query_maps, key_map, linear_cotangent):
    tokens_here, hd = keys.shape
    heads = queries.shape[1]
    count = lax.axis_size("seq")
    inner = 2 if heads % 2 == 0 else 1
    outer = heads // inner
    share = hd // count
    tiles = 4
    rows_sub = min(512, TILE * heads)
    step_rows = TILE * tiles * heads
    total = tokens_here * heads
    steps = total // step_rows
    early = steps // 4
    late_tiles = (steps - early) * tiles // steps
    late_rows = late_tiles * TILE * heads
    whole = lambda a: pl.BlockSpec(a.shape, lambda i: (0,) * len(a.shape))
    rows_spec = pl.BlockSpec((step_rows, hd), lambda i: (i, 0))
    maps = query_maps.reshape(heads * hd, hd)
    queries = queries.reshape(total, hd)
    cotangent = linear_cotangent.reshape(total, hd)

    rows16 = jax.ShapeDtypeStruct((total, hd), jnp.bfloat16)
    late16 = jax.ShapeDtypeStruct((steps * late_rows, hd), jnp.bfloat16)
    kf16 = jax.ShapeDtypeStruct((tokens_here, hd), jnp.bfloat16)
    rim = jax.ShapeDtypeStruct((W, hd), jnp.bfloat16)
    square = jax.ShapeDtypeStruct((hd, hd), jnp.float32)
    dma = pltpu.SemaphoreType.DMA
    query_features, late_soft, key_features, rim_keys, rim_values, prefix = pl.pallas_call(
        functools.partial(first_kernel, count, heads, inner, steps, early * tiles, late_tiles),
        grid=(steps,),
        in_specs=[rows_spec]
        + [
            pl.BlockSpec((TILE * heads, hd), lambda i, j=j: (early * tiles + i * late_tiles + j, 0))
            for j in range(late_tiles)
        ]
        + [whole(a) for a in (maps, keys, values, key_map)],
        out_specs=[rows_spec, pl.BlockSpec((late_rows, hd), lambda i: (i, 0))]
        + [whole(a) for a in (kf16, rim, rim, square)],
        out_shape=[rows16, late16, kf16, rim, rim, square],
        scratch_shapes=[
            pltpu.VMEM((tokens_here, 2 * hd), jnp.bfloat16),
            pltpu.VMEM((rows_sub, outer * hd), jnp.bfloat16),
            pltpu.VMEM((hd, hd), jnp.float32),
            pltpu.VMEM((count - 1, hd, hd), jnp.float32),
            pltpu.VMEM((2, W, hd), jnp.bfloat16),
            dma((count - 1,)), dma((count - 1,)), dma((2,)), dma((2,)),
        ],
        compiler_params=pltpu.CompilerParams(
            dimension_semantics=("arbitrary",), collective_id=0, has_side_effects=True
        ),
        name="features",
    )(queries, *[queries] * late_tiles, maps, keys, values, key_map)

    pieces = (count, share, heads * hd)
    small = (keys, values, key_features, rim_keys, rim_values, prefix)
    soft, linear, grad, grad16 = pl.pallas_call(
        functools.partial(main_kernel, tokens_here, heads, inner, tiles, rows_sub, steps, early),
        grid=(steps,),
        in_specs=[rows_spec] * 3
        + [pl.BlockSpec((step_rows, hd), lambda i: (jnp.maximum(i - early, 0), 0))]
        + [whole(a) for a in small],
        out_specs=[rows_spec] * 2 + [pl.BlockSpec(pieces, lambda i: (0, 0, 0))] * 2,
        out_shape=[
            rows16, rows16,
            jax.ShapeDtypeStruct(pieces, jnp.float32),
            jax.ShapeDtypeStruct(pieces, jnp.bfloat16),
        ],
        scratch_shapes=[
            pltpu.VMEM((tokens_here + W, hd), jnp.bfloat16),
            pltpu.VMEM((tokens_here + W, 2 * hd), jnp.bfloat16),
            pltpu.VMEM((rows_sub, outer * hd), jnp.bfloat16),
            pltpu.VMEM((rows_sub, inner * hd), jnp.bfloat16),
            pltpu.VMEM((hd, hd), jnp.float32),
            pltpu.VMEM((outer * hd, inner * hd), jnp.float32),
        ],
        compiler_params=pltpu.CompilerParams(dimension_semantics=("arbitrary",)),
        name="attention",
    )(queries, query_features, cotangent, late_soft, *small)

    vmem = pl.BlockSpec(memory_space=pltpu.VMEM)
    mine = pl.pallas_call(
        functools.partial(last_kernel, count),
        in_specs=[vmem, vmem],
        out_specs=vmem,
        out_shape=jax.ShapeDtypeStruct((share, heads, hd), jnp.float32),
        scratch_shapes=[
            pltpu.VMEM((count - 1,) + pieces[1:], jnp.bfloat16), dma((count - 1,)), dma((count - 1,)),
        ],
        compiler_params=pltpu.CompilerParams(collective_id=1, has_side_effects=True),
        name="map_gradient",
    )(grad, grad16)
    shape = (tokens_here, heads, hd)
    return soft.reshape(shape), linear.reshape(shape), mine


def solution(mesh):
    rows = P(("groups", "seq"), ("head", "rep"), None)
    return jax.shard_map(
        per_device,
        mesh=mesh,
        in_specs=(
            rows,
            P(("groups", "seq"), None),
            P(("groups", "seq"), None),
            P(("groups", "head", "rep"), None, None),
            P("groups", None),
            rows,
        ),
        out_specs=(rows, rows, rows),
        check_vma=False,
    )
```
